32 devices in a mesh: wide: 8 (over z, y), narrow: 4 (over x, core).
Axes of the slice: x: 2, y: 2, z: 4, core: 2. Of those that a mesh axis runs over, the one named last changes fastest.
Arguments:
- block_input: bfloat16 [8256, 1152], P(('wide', 'narrow')), may hold values from -6 to 6
- skip_input: bfloat16 [8256, 1152], P(('wide', 'narrow')), may hold values from -6 to 6
- out_grad: bfloat16 [8256, 1152], P(('wide', 'narrow')), may hold values from -6 to 6
- skip_weight: bfloat16 [2654208], P(('wide', 'narrow')), may hold values from -0.125 to 0.125
- qkv_weight: bfloat16 [3981312], P(('wide', 'narrow')), may hold values from -0.1875 to 0.1875
- proj_weight: bfloat16 [1327104], P(('wide', 'narrow')), may hold values from -0.5 to 0.5
- up_weight: bfloat16 [5308416], P(('wide', 'narrow')), may hold values from -0.1875 to 0.1875
- down_weight: bfloat16 [5308416], P(('wide', 'narrow')), may hold values from -0.09375 to 0.09375
- gains: float32 [2, 1152], P(None, 'narrow'), may hold values from 0.5 to 1.5
- biases: float32 [5, 1152], P(None, 'narrow'), may hold values from -3 to 3
- up_bias: float32 [4608], P('narrow'), may hold values from -3 to 3
Outputs:
- block_output: bfloat16 [8256, 1152], P(('wide', 'narrow'))
- input_grad: float32 [8256, 1152], P(('wide', 'narrow'))
- skip_grad: float32 [8256, 1152], P(('wide', 'narrow'))
- skip_weight_grad: float32 [2654208], P(('wide', 'narrow'))
- qkv_weight_grad: float32 [3981312], P(('wide', 'narrow'))
- proj_weight_grad: float32 [1327104], P(('wide', 'narrow'))
- up_weight_grad: float32 [5308416], P(('wide', 'narrow'))
- down_weight_grad: float32 [5308416], P(('wide', 'narrow'))
- gains_grad: float32 [2, 1152], P(None, 'narrow')
- biases_grad: float32 [5, 1152], P(None, 'narrow')
- up_bias_grad: float32 [4608], P('narrow')
The draws below stay inside these ranges and needn't reach their ends.
All inputs are finite; a program needn't handle non-finite values.
Results may differ from the reference program's by a relative error of at most 0.009.
Values may be sent and summed in bfloat16 or wider, within the bound.
No kernel may reach another device: no remote copies, remote signals or barrier semaphores. Data moves between devices by JAX's collectives and lax.ppermute only.
A program may use at most 384 MiB of HBM per device.

```python
import math
import jax
import jax.numpy as jnp
from jax import lax

D = 1152
HEADS = 16
HD = 72
FF = 4608
SEQ = 258
IMAGES = 32
ROWS = 8256


def strengthened(array, key, source, target, shards_of, factor):
    def block_of(dim):
        return (jnp.arange(array.shape[dim]) // (array.shape[dim] // shards_of)).reshape((-1,) + (1,) * (array.ndim - 1 - dim))

    first = jax.random.permutation(key, shards_of)[block_of(target)]
    other_side = (block_of(target) + shards_of // 2) % shards_of
    return jnp.where((block_of(source) == first) | (block_of(source) == other_side), factor * array, array)


def block_scale(stream_key, dims, shards, least, top_value):
    loudness = 1.0
    for dim, blocks in shards:
        steps = jax.random.uniform(jax.random.fold_in(jax.random.fold_in(stream_key, 6), dim), (blocks,), jnp.float32, least / len(shards), top_value / len(shards))
        loudness = loudness * jnp.repeat(jnp.exp(steps), dims[dim] // blocks).reshape((-1,) + (1,) * (len(dims) - 1 - dim))
    return loudness


def normal_values(key, extent, width, most, split=(), held_as=jnp.bfloat16):
    array = width * jax.random.normal(key, extent, jnp.float32)
    if split:
        array = array * block_scale(key, extent, split, -0.22, 0.18)
    return jnp.clip(array, -most, most).astype(held_as)


def bell_draw_with(key, extent, scale, limit, cuts, heavy, kind=jnp.bfloat16):
    entries = scale * jax.random.normal(key, extent, jnp.float32)
    if cuts:
        entries = entries * block_scale(key, extent, cuts, -0.22, 0.18)
    return jnp.clip(strengthened(entries, jax.random.fold_in(key, 3), *heavy), -limit, limit).astype(kind)


def setup_inputs(seed: int = 0) -> dict:
    seeds = jax.random.split(jax.random.key(seed), 12)
    return {
        "block_input": normal_values(seeds[0], (ROWS, D), 1.0, 6.0, ((0, 32),)),
        "skip_input": normal_values(seeds[1], (ROWS, D), 1.0, 6.0, ((0, 32),)),
        "out_grad": bell_draw_with(seeds[2], (ROWS, D), 1.0, 6.0, ((0, 32),), (0, 1, 32, 2.75)),
        "skip_weight": normal_values(seeds[3], (2 * D * D,), (2 * D) ** -0.5, 0.125, ((0, 32),)),
        "qkv_weight": normal_values(seeds[4], (3 * D * D,), D ** -0.5, 0.1875, ((0, 32),)),
        "proj_weight": normal_values(seeds[5], (D * D,), (D // 8) ** -0.5, 0.5, ((0, 32),)),
        "up_weight": normal_values(seeds[6], (D * FF,), D ** -0.5, 0.1875, ((0, 32),)),
        "down_weight": normal_values(seeds[7], (FF * D,), FF ** -0.5, 0.09375, ((0, 32),)),
        "gains": jnp.clip(1.0 + 0.1 * jax.random.normal(seeds[8], (2, D), jnp.float32), 0.5, 1.5),
        "biases": normal_values(seeds[9], (5, D), 0.5, 3.0, ((1, 4),), jnp.float32),
        "up_bias": normal_values(seeds[10], (FF,), 0.5, 3.0, ((0, 4),), jnp.float32),
    }


@jax.custom_vjp
def low(v):
    return lax.optimization_barrier(v.astype(jnp.bfloat16)).astype(jnp.float32)

@jax.custom_vjp
def low_back(v):
    return v

def low_keep(v):
    return (low(v), None)

def low_pass(kept, grad):
    return (grad,)

def back_keep(v):
    return (v, None)

def back_low(kept, grad):
    return (low(grad),)
low.defvjp(low_keep, low_pass)
low_back.defvjp(back_keep, back_low)
highest = lax.Precision.HIGHEST
eps_norm = 1e-05

def layer_norm(values, gain_vec, offset):
    row_mean = lax.optimization_barrier(jnp.mean(values, axis=-1, keepdims=True))
    centered = values - row_mean
    variance = lax.optimization_barrier(jnp.mean(centered * centered, axis=-1, keepdims=True))
    return centered * lax.rsqrt(variance + eps_norm) * gain_vec + offset

def exact_gelu(values):
    return jax.nn.gelu(values, approximate=False)

def images_forward(inputs, skip_rows, matrices, gain_rows, bias_rows, hidden_bias):
    skip_mat, qkv_mat, proj_mat, up_mat, down_mat = matrices
    group_size, seq_len = (inputs.shape[0], inputs.shape[1])
    stacked = jnp.concatenate([inputs, skip_rows], axis=-1)
    joined = low_back(jnp.einsum('gsc,cd->gsd', stacked, skip_mat, precision=highest) + bias_rows[0])
    normed = low(layer_norm(joined, gain_rows[0], bias_rows[1]))
    projected = low_back(low(jnp.einsum('gsd,de->gse', normed, qkv_mat, precision=highest)))
    split_heads = projected.reshape(group_size, seq_len, 3, HEADS, HD)
    queries = split_heads[:, :, 0]
    keys_all = split_heads[:, :, 1]
    values_all = split_heads[:, :, 2]
    raw_scores = jnp.einsum('gqhd,gkhd->ghqk', queries, keys_all, precision=highest)
    scores = low_back(raw_scores * HD ** (-0.5))
    probabilities = low(jax.nn.softmax(scores, axis=-1))
    attended = jnp.einsum('ghqk,gkhd->gqhd', probabilities, values_all, precision=highest)
    attended = low(low_back(attended)).reshape(group_size, seq_len, HEADS * HD)
    branch = low_back(jnp.einsum('gsd,de->gse', attended, proj_mat, precision=highest) + bias_rows[2])
    middle = joined + branch
    normed_mid = low(layer_norm(middle, gain_rows[1], bias_rows[3]))
    pre_act = low_back(jnp.einsum('gsd,df->gsf', normed_mid, up_mat, precision=highest) + hidden_bias)
    activated = low(exact_gelu(pre_act))
    ff_branch = low_back(jnp.einsum('gsf,fd->gsd', activated, down_mat, precision=highest) + bias_rows[4])
    return middle + ff_branch

def reference(block_input, skip_input, out_grad, skip_weight, qkv_weight, proj_weight, up_weight, down_weight, gains, biases, up_bias):

    def to_images(row_array):
        return row_array.astype(jnp.float32).reshape(IMAGES, SEQ, D)

    def to_rows(images):
        return images.reshape(ROWS, D)
    group_size = math.gcd(IMAGES, 16)
    group_count = IMAGES // group_size

    def whole(inputs, skip_rows, matrices, gain_rows, bias_rows, hidden_bias):

        def one_group(group_pair):
            return images_forward(group_pair[0], group_pair[1], matrices, gain_rows, bias_rows, hidden_bias)
        outcome = lax.map(jax.checkpoint(one_group), (inputs.reshape(group_count, group_size, SEQ, D), skip_rows.reshape(group_count, group_size, SEQ, D)))
        return outcome.reshape(IMAGES, SEQ, D)
    matrices = (skip_weight.astype(jnp.float32).reshape(2 * D, D), qkv_weight.astype(jnp.float32).reshape(D, 3 * D), proj_weight.astype(jnp.float32).reshape(D, D), up_weight.astype(jnp.float32).reshape(D, FF), down_weight.astype(jnp.float32).reshape(FF, D))
    result, pullback = jax.vjp(whole, to_images(block_input), to_images(skip_input), matrices, gains.astype(jnp.float32), biases.astype(jnp.float32), up_bias.astype(jnp.float32))
    gradients = pullback(to_images(out_grad))
    input_grad, skip_grad, matrix_grads, gains_grad, biases_grad, up_bias_grad = gradients
    return (to_rows(result).astype(jnp.bfloat16), to_rows(input_grad), to_rows(skip_grad), matrix_grads[0].reshape(-1), matrix_grads[1].reshape(-1), matrix_grads[2].reshape(-1), matrix_grads[3].reshape(-1), matrix_grads[4].reshape(-1), gains_grad, biases_grad, up_bias_grad)
```

```python
import functools
import math

import jax
import jax.numpy as jnp
from jax import lax
from jax.experimental import pallas as pl
from jax.experimental.pallas import tpu as pltpu
from jax.sharding import PartitionSpec as P

HD = 72
SEQ = 258


eps_norm = 1e-05


def layer_norm(values, gain_vec, offset):
    row_mean = jnp.mean(values, axis=-1, keepdims=True)
    centered = values - row_mean
    variance = jnp.mean(centered * centered, axis=-1, keepdims=True)
    return centered * lax.rsqrt(variance + eps_norm) * gain_vec + offset


def exact_gelu(values):
    return jax.nn.gelu(values, approximate=False)


def shaped(gathered, model_width, hidden):
    return (
        gathered[0].reshape(2 * model_width, model_width),
        gathered[1].reshape(model_width, 3 * model_width),
        gathered[2].reshape(model_width, model_width),
        gathered[3].reshape(model_width, hidden),
        gathered[4].reshape(hidden, model_width),
    )


def times_transposed(left, right):
    return jnp.einsum("rf,cf->rc", left, right, preferred_element_type=jnp.float32)


def inner_rows(left, right):
    return jnp.einsum("rc,rd->cd", left, right, preferred_element_type=jnp.float32)


def shards(
    block_input,
    skip_input,
    out_grad,
    skip_weight,
    qkv_weight,
    proj_weight,
    up_weight,
    down_weight,
    gains,
    biases,
    up_bias,
):
    row_count, model_width = block_input.shape
    images_here = row_count // SEQ
    head_count = model_width // HD
    score_scale = HD ** (-0.5)
    gathered = (
        lax.all_gather(skip_weight, ("wide", "narrow"), axis=0, tiled=True),
        lax.all_gather(qkv_weight, ("wide", "narrow"), axis=0, tiled=True),
        lax.all_gather(proj_weight, ("wide", "narrow"), axis=0, tiled=True),
        lax.all_gather(up_weight, ("wide", "narrow"), axis=0, tiled=True),
        lax.all_gather(down_weight, ("wide", "narrow"), axis=0, tiled=True),
    )
    vectors = (
        lax.all_gather(gains, "narrow", axis=1, tiled=True),
        lax.all_gather(biases, "narrow", axis=1, tiled=True),
        lax.all_gather(up_bias, "narrow", axis=0, tiled=True),
    )
    gain_all, bias_all, up_bias_all = vectors
    hidden = up_bias_all.shape[0]
    skip_mat, qkv_mat, proj_mat, up_mat, down_mat = shaped(gathered, model_width, hidden)
    stacked = jnp.concatenate([block_input, skip_input], axis=1)
    joined = jnp.dot(stacked, skip_mat, preferred_element_type=jnp.float32) + bias_all[0]
    normed, norm_back = jax.vjp(layer_norm, joined, gain_all[0], bias_all[1])
    normed_low = normed.astype(jnp.bfloat16)
    projected = jnp.dot(normed_low, qkv_mat, preferred_element_type=jnp.float32).astype(
        jnp.bfloat16
    )
    queries = projected[:, :model_width].reshape(images_here, SEQ, head_count, HD)
    keys_all = projected[:, model_width : 2 * model_width].reshape(images_here, SEQ, head_count, HD)
    values_all = projected[:, 2 * model_width :].reshape(images_here, SEQ, head_count, HD)
    scores = (
        jnp.einsum("iqhd,ikhd->ihqk", queries, keys_all, preferred_element_type=jnp.float32)
        * score_scale
    )
    row_max = jnp.max(scores, axis=-1, keepdims=True)
    exp_scores = jnp.exp(scores - row_max)
    row_sum = jnp.sum(exp_scores, axis=-1, keepdims=True)
    probabilities = exp_scores / row_sum
    row_lse = row_max + jnp.log(row_sum)
    probs_low = probabilities.astype(jnp.bfloat16)
    attended = jnp.einsum(
        "ihqk,ikhd->iqhd", probs_low, values_all, preferred_element_type=jnp.float32
    )
    attended = attended.astype(jnp.bfloat16).reshape(row_count, model_width)
    middle = joined + (
        jnp.dot(attended, proj_mat, preferred_element_type=jnp.float32) + bias_all[2]
    )
    normed_mid, norm_mid_back = jax.vjp(layer_norm, middle, gain_all[1], bias_all[3])
    normed_mid_low = normed_mid.astype(jnp.bfloat16)
    pre_act = jnp.dot(normed_mid_low, up_mat, preferred_element_type=jnp.float32) + up_bias_all
    activated, gelu_back = jax.vjp(exact_gelu, pre_act)
    activated_low = activated.astype(jnp.bfloat16)
    block_output = middle + (
        jnp.dot(activated_low, down_mat, preferred_element_type=jnp.float32) + bias_all[4]
    )
    down_flat = inner_rows(activated_low, out_grad).reshape(-1)
    down_bias_grad = jnp.sum(out_grad.astype(jnp.float32), axis=0)
    activated_grad = times_transposed(out_grad, down_mat)
    pre_grad = gelu_back(activated_grad)[0].astype(jnp.bfloat16)
    up_flat = inner_rows(normed_mid_low, pre_grad).reshape(-1)
    up_bias_grad = jnp.sum(pre_grad.astype(jnp.float32), axis=0)
    normed_mid_grad = times_transposed(pre_grad, up_mat)
    middle_from_norm, gain_mid_grad, offset_mid_grad = norm_mid_back(normed_mid_grad)
    middle_grad = out_grad.astype(jnp.float32) + middle_from_norm
    branch_grad = middle_grad.astype(jnp.bfloat16)
    proj_flat = inner_rows(attended, branch_grad).reshape(-1)
    proj_bias_grad = jnp.sum(branch_grad.astype(jnp.float32), axis=0)
    attended_grad = times_transposed(branch_grad, proj_mat)
    attended_grad = attended_grad.astype(jnp.bfloat16).reshape(images_here, SEQ, head_count, HD)
    scores_again = (
        jnp.einsum("iqhd,ikhd->ihqk", queries, keys_all, preferred_element_type=jnp.float32)
        * score_scale
    )
    probs_again = jnp.exp(scores_again - row_lse)
    probs_again_low = probs_again.astype(jnp.bfloat16)
    prob_grad = jnp.einsum(
        "iqhd,ikhd->ihqk", attended_grad, values_all, preferred_element_type=jnp.float32
    )
    value_grad = jnp.einsum(
        "ihqk,iqhd->ikhd", probs_again_low, attended_grad, preferred_element_type=jnp.float32
    )
    inner_sum = jnp.sum(prob_grad * probs_again, axis=-1, keepdims=True)
    score_grad = (probs_again * (prob_grad - inner_sum)).astype(jnp.bfloat16)
    query_grad = (
        jnp.einsum("ihqk,ikhd->iqhd", score_grad, keys_all, preferred_element_type=jnp.float32)
        * score_scale
    )
    key_grad = (
        jnp.einsum("ihqk,iqhd->ikhd", score_grad, queries, preferred_element_type=jnp.float32)
        * score_scale
    )
    projected_grad = jnp.concatenate(
        [
            query_grad.reshape(row_count, model_width),
            key_grad.reshape(row_count, model_width),
            value_grad.reshape(row_count, model_width),
        ],
        axis=1,
    ).astype(jnp.bfloat16)
    qkv_flat = inner_rows(normed_low, projected_grad).reshape(-1)
    normed_grad = times_transposed(projected_grad, qkv_mat)
    joined_from_norm, gain_first_grad, offset_first_grad = norm_back(normed_grad)
    joined_grad = (middle_grad + joined_from_norm).astype(jnp.bfloat16)
    skip_flat = inner_rows(stacked, joined_grad).reshape(-1)
    skip_bias_grad = jnp.sum(joined_grad.astype(jnp.float32), axis=0)
    both_grads = times_transposed(joined_grad, skip_mat)
    input_grad = both_grads[:, :model_width]
    skip_grad = both_grads[:, model_width:]
    gain_grads = jnp.stack([gain_first_grad, gain_mid_grad])
    bias_grads = jnp.stack(
        [skip_bias_grad, offset_first_grad, proj_bias_grad, offset_mid_grad, down_bias_grad]
    )
    vector_sums = lax.psum((gain_grads, bias_grads, up_bias_grad), ("wide", "narrow"))
    narrow_count = lax.axis_size("narrow")
    place = lax.axis_index("narrow")
    width_part = model_width // narrow_count
    hidden_part = hidden // narrow_count
    gains_grad = lax.dynamic_slice_in_dim(vector_sums[0], place * width_part, width_part, 1)
    biases_grad = lax.dynamic_slice_in_dim(vector_sums[1], place * width_part, width_part, 1)
    up_bias_sum = lax.dynamic_slice_in_dim(vector_sums[2], place * hidden_part, hidden_part, 0)
    matrix_sums = (
        lax.psum_scatter(skip_flat, ("wide", "narrow"), scatter_dimension=0, tiled=True),
        lax.psum_scatter(qkv_flat, ("wide", "narrow"), scatter_dimension=0, tiled=True),
        lax.psum_scatter(proj_flat, ("wide", "narrow"), scatter_dimension=0, tiled=True),
        lax.psum_scatter(up_flat, ("wide", "narrow"), scatter_dimension=0, tiled=True),
        lax.psum_scatter(down_flat, ("wide", "narrow"), scatter_dimension=0, tiled=True),
    )
    return (
        block_output.astype(jnp.bfloat16),
        input_grad,
        skip_grad,
        matrix_sums[0],
        matrix_sums[1],
        matrix_sums[2],
        matrix_sums[3],
        matrix_sums[4],
        gains_grad,
        biases_grad,
        up_bias_sum,
    )


AXES = ("wide", "narrow")
DEVICES = 32


def flipped(bits_core0, bits_core1):
    return [
        (device, device ^ (bits_core1 if device & 1 else bits_core0)) for device in range(DEVICES)
    ]


TO_CORE = flipped(1, 1)
TO_Z = [flipped(8 * step, 8 * step) for step in range(4)]
TO_NEAR = flipped(4, 2)
TO_FAR = flipped(2, 4)
TO_X = flipped(2, 2)
TO_Y = flipped(4, 4)


def send(value, pairs):
    return lax.ppermute(value, AXES, pairs)


def places():
    device = lax.axis_index("wide") * 4 + lax.axis_index("narrow")
    core = device & 1
    return device, core


def spread(block):
    group = jnp.stack([block] + [send(block, TO_Z[step]) for step in (1, 2, 3)])
    group = jnp.concatenate([group, send(group, TO_NEAR)], 0)
    other = send(group, TO_FAR)
    return group, other, send(group, TO_CORE), send(other, TO_CORE)


def gather_copies(by_rows, pieces, held, sems):
    device = lax.axis_index("wide") * 4 + lax.axis_index("narrow")
    core = device % 2
    chip = device // 2
    z, y, x = chip // 4, (chip // 2) % 2, chip % 2
    own, theirs = pieces[:2], pieces[2:]
    part = pieces[0].shape[-1]
    rest = held.shape[-1] - part
    copies = []
    for far in range(2):
        for near in range(2):
            flip_y = near * (1 - core) + far * core
            flip_x = far * (1 - core) + near * core
            corner = ((y + flip_y) % 2) * 2 + (x + flip_x) % 2
            for step in range(4):
                z_high, z_low = z // 2, z % 2
                z_high = 1 - z_high if step & 2 else z_high
                z_low = 1 - z_low if step & 1 else z_low
                place = (z_high * 2 + z_low) * 4 + corner
                mine = own[far].at[near * 4 + step]
                other = theirs[near].at[far * 4 + step]
                if by_rows:
                    to_mine = held.at[place, core]
                    to_other = held.at[place, 1 - core]
                else:
                    from_other = pl.multiple_of((1 - core) * (part - rest), 128)
                    other = other.at[:, pl.ds(from_other, rest)]
                    to_mine = held.at[place, :, pl.ds(pl.multiple_of(core * rest, 128), part)]
                    to_other = held.at[
                        place, :, pl.ds(pl.multiple_of((1 - core) * part, 128), rest)
                    ]
                n = 2 * len(copies)
                copies.append(
                    (
                        place,
                        pltpu.make_async_copy(mine, to_mine, sems.at[n]),
                        pltpu.make_async_copy(other, to_other, sems.at[n + 1]),
                    )
                )
    return copies


def assemble_kernel(by_rows, *refs):
    pieces, (out_ref, held, sem_in, sem_out) = refs[:4], refs[4:]
    copies = gather_copies(by_rows, pieces, held, sem_in)
    for _, mine, other in copies:
        mine.start()
        other.start()
    outs = []
    for n, (place, mine, other) in enumerate(copies):
        mine.wait()
        other.wait()
        out = pltpu.make_async_copy(held.at[place], out_ref.at[place], sem_out.at[n])
        out.start()
        outs.append(out)
    for out in outs:
        out.wait()


def assemble(pieces, rows, width, by_rows):
    shape = (16, 2, rows, width) if by_rows else (16, rows, width)
    size = 2 * math.prod(shape)
    out = pl.pallas_call(
        functools.partial(assemble_kernel, by_rows),
        out_shape=jax.ShapeDtypeStruct(shape, jnp.bfloat16),
        in_specs=[pl.BlockSpec(memory_space=pl.ANY)] * 4,
        out_specs=pl.BlockSpec(memory_space=pl.ANY),
        scratch_shapes=[
            pltpu.VMEM(shape, jnp.bfloat16),
            pltpu.SemaphoreType.DMA((32,)),
            pltpu.SemaphoreType.DMA((16,)),
        ],
        cost_estimate=pl.CostEstimate(flops=0, bytes_accessed=2 * size, transcendentals=0),
        name="assemble",
    )(*pieces)
    return out.reshape(-1, width)


def fold(kept, sent_to_core, chip, core):
    f32 = jnp.float32
    bf16 = jnp.bfloat16
    corner = chip % 4
    z = chip // 4
    near_bit = 2 - core
    far_bit = 1 + core
    from_core = send(sent_to_core, TO_CORE)

    def at(bits):
        blocks = lax.dynamic_index_in_dim(from_core, corner ^ bits, 1, keepdims=False)
        return kept(0, 4, corner ^ bits).astype(f32) + blocks.astype(f32)

    to_far = jnp.stack([at(far_bit), at(far_bit | near_bit)]).astype(bf16)
    from_far = send(to_far, TO_FAR)
    to_near = (at(near_bit) + from_far[1].astype(f32)).astype(bf16)
    from_near = send(to_near, TO_NEAR)

    def total(place):
        blocks = [
            kept(place, 1, corner)[0],
            lax.dynamic_slice(
                from_core, (place, corner, 0, 0), (1, 1) + from_core.shape[2:]
            )[0, 0],
            lax.dynamic_index_in_dim(from_far[0], place, 0, keepdims=False),
            lax.dynamic_index_in_dim(from_near, place, 0, keepdims=False),
        ]
        blocks = [b.astype(f32) for b in blocks]
        return (blocks[0] + blocks[1]) + (blocks[2] + blocks[3])

    arrived = [send(total(z ^ step).astype(bf16), TO_Z[step]) for step in (1, 2, 3)]
    return total(z) + sum(a.astype(f32) for a in arrived)


def fold_rows(blocks, chip, core):
    def kept(start, count, corner):
        shape = (count, 1, 1) + blocks.shape[3:]
        return lax.dynamic_slice(blocks, (start, corner, core, 0, 0), shape)[:, 0, 0]

    theirs = lax.dynamic_index_in_dim(blocks, 1 - core, 2, keepdims=False)
    return fold(kept, theirs, chip, core).reshape(-1)


def half_columns(array, whose, part):
    start = whose * (array.shape[1] - part)
    return lax.dynamic_slice_in_dim(array, start, part, 1)


def join_columns(summed, core, width, rows):
    part = summed.shape[1]
    mine = lax.dynamic_slice_in_dim(summed, core * rows, rows, 0)
    other = send(lax.dynamic_slice_in_dim(summed, (1 - core) * rows, rows, 0), TO_CORE)
    rest = width - part
    first = jnp.concatenate([mine, other[:, part - rest :]], 1)
    second = jnp.concatenate([other[:, :rest], mine], 1)
    return jnp.where(core == 0, first, second).reshape(-1)


def gathered_vectors(gains, biases, up_bias, core, x):
    flat = jnp.concatenate([gains.reshape(-1), biases.reshape(-1), up_bias])[None]

    def both(mine, other, place):
        return jnp.where(
            place == 0, jnp.concatenate([mine, other], 0), jnp.concatenate([other, mine], 0)
        )

    flat = both(flat, send(flat, TO_CORE), core)
    everyone = both(flat, send(flat, TO_X), x)
    width = gains.shape[1]
    gain_all = everyone[:, : 2 * width].reshape(4, 2, width).transpose(1, 0, 2).reshape(2, 4 * width)
    bias_all = (
        everyone[:, 2 * width : 7 * width].reshape(4, 5, width).transpose(1, 0, 2).reshape(5, 4 * width)
    )
    return gain_all, bias_all, everyone[:, 7 * width :].reshape(-1)


def vector_total(gain_grads, bias_grads, up_bias_grad, device):
    width = gain_grads.shape[1] // 4
    rows = jnp.concatenate([gain_grads, bias_grads], 0).reshape(7, 4, width).transpose(1, 0, 2)
    packed = jnp.concatenate([rows.reshape(4, 7 * width), up_bias_grad.reshape(4, -1)], 1)
    core = device & 1
    x = (device >> 1) & 1
    packed = packed.reshape(2, 2, -1)

    def take(array, index, dim):
        return lax.dynamic_index_in_dim(array, index, dim, keepdims=False)

    packed = take(packed, core, 1) + send(take(packed, 1 - core, 1), TO_CORE)
    packed = take(packed, x, 0) + send(take(packed, 1 - x, 0), TO_X)
    for pairs in (TO_Y, TO_Z[1], TO_Z[2]):
        packed = packed + send(packed, pairs)
    return (
        packed[: 2 * width].reshape(2, width),
        packed[2 * width : 7 * width].reshape(5, width),
        packed[7 * width :],
    )


def padded_half(width):
    return -(-width // 256) * 128


def fast_shards(
    block_input,
    skip_input,
    out_grad,
    skip_weight,
    qkv_weight,
    proj_weight,
    up_weight,
    down_weight,
    gains,
    biases,
    up_bias,
):
    row_count, model_width = block_input.shape
    hidden = 4 * up_bias.shape[0]
    device, core = places()
    chip = device // 2
    images_here = row_count // SEQ
    head_count = model_width // HD
    score_scale = HD ** (-0.5)
    bf16 = jnp.bfloat16

    gain_all, bias_all, up_bias_all = gathered_vectors(gains, biases, up_bias, core, chip % 2)
    rows = model_width // DEVICES
    skip_pieces = spread(skip_weight.reshape(2 * rows, model_width))
    wide_mats = [
        qkv_weight.reshape(rows, 3 * model_width),
        proj_weight.reshape(rows, model_width),
        up_weight.reshape(rows, hidden),
    ]
    parts = [padded_half(m.shape[1]) for m in wide_mats]
    mine = jnp.concatenate([half_columns(m, core, p) for m, p in zip(wide_mats, parts)], 1)
    others = send(
        jnp.concatenate([half_columns(m, 1 - core, p) for m, p in zip(wide_mats, parts)], 1), TO_CORE
    )
    chip_rows = jnp.where(
        core == 0, jnp.concatenate([mine, others], 0), jnp.concatenate([others, mine], 0)
    )
    qkv_pieces = spread(chip_rows[:, : parts[0]])
    proj_pieces = spread(chip_rows[:, parts[0] : parts[0] + parts[1]])
    up_pieces = spread(chip_rows[:, parts[0] + parts[1] :])
    down_pieces = spread(down_weight.reshape(4 * rows, model_width))

    skip_mat = assemble(skip_pieces, 2 * rows, model_width, True)
    qkv_mat = assemble(qkv_pieces, 2 * rows, 3 * model_width, False)
    proj_mat = assemble(proj_pieces, 2 * rows, model_width, False)
    up_mat = assemble(up_pieces, 2 * rows, hidden, False)
    down_mat = assemble(down_pieces, 4 * rows, model_width, True)

    stacked = jnp.concatenate([block_input, skip_input], axis=1)
    joined = jnp.dot(stacked, skip_mat, preferred_element_type=jnp.float32) + bias_all[0]
    normed, norm_back = jax.vjp(layer_norm, joined, gain_all[0], bias_all[1])
    normed_low = normed.astype(bf16)
    projected = jnp.dot(normed_low, qkv_mat, preferred_element_type=jnp.float32).astype(bf16)
    queries = projected[:, :model_width].reshape(images_here, SEQ, head_count, HD)
    keys_all = projected[:, model_width : 2 * model_width].reshape(images_here, SEQ, head_count, HD)
    values_all = projected[:, 2 * model_width :].reshape(images_here, SEQ, head_count, HD)
    scores = (
        jnp.einsum("iqhd,ikhd->ihqk", queries, keys_all, preferred_element_type=jnp.float32)
        * score_scale
    )
    row_max = jnp.max(scores, axis=-1, keepdims=True)
    exp_scores = jnp.exp(scores - row_max)
    row_sum = jnp.sum(exp_scores, axis=-1, keepdims=True)
    probabilities = exp_scores / row_sum
    row_lse = row_max + jnp.log(row_sum)
    probs_low = probabilities.astype(bf16)
    attended = jnp.einsum(
        "ihqk,ikhd->iqhd", probs_low, values_all, preferred_element_type=jnp.float32
    )
    attended = attended.astype(bf16).reshape(row_count, model_width)
    middle = joined + (
        jnp.dot(attended, proj_mat, preferred_element_type=jnp.float32) + bias_all[2]
    )
    normed_mid, norm_mid_back = jax.vjp(layer_norm, middle, gain_all[1], bias_all[3])
    normed_mid_low = normed_mid.astype(bf16)
    pre_act = jnp.dot(normed_mid_low, up_mat, preferred_element_type=jnp.float32) + up_bias_all
    activated, gelu_back = jax.vjp(exact_gelu, pre_act)
    activated_low = activated.astype(bf16)

    down_blocks = inner_rows(activated_low, out_grad).astype(bf16).reshape(4, 4, 2, 4 * rows, model_width)
    down_total = fold_rows(down_blocks, chip, core)
    block_output = middle + (
        jnp.dot(activated_low, down_mat, preferred_element_type=jnp.float32) + bias_all[4]
    )
    down_bias_grad = jnp.sum(out_grad.astype(jnp.float32), axis=0)
    activated_grad = times_transposed(out_grad, down_mat)
    pre_grad = gelu_back(activated_grad)[0].astype(bf16)

    def by_columns(left, right, part):
        def one(whose):
            return (
                inner_rows(left, half_columns(right, whose, part))
                .astype(bf16)
                .reshape(4, 4, 2 * rows, part)
            )

        width = right.shape[1]
        theirs = one(1 - core)
        mine = one(core)

        def kept(start, count, corner):
            return lax.dynamic_slice(mine, (start, corner, 0, 0), (count, 1) + mine.shape[2:])[:, 0]

        return join_columns(fold(kept, theirs, chip, core), core, width, rows)

    up_total = by_columns(normed_mid_low, pre_grad, parts[2])
    up_bias_grad = jnp.sum(pre_grad.astype(jnp.float32), axis=0)
    normed_mid_grad = times_transposed(pre_grad, up_mat)
    middle_from_norm, gain_mid_grad, offset_mid_grad = norm_mid_back(normed_mid_grad)
    middle_grad = out_grad.astype(jnp.float32) + middle_from_norm
    branch_grad = middle_grad.astype(bf16)
    proj_total = by_columns(attended, branch_grad, parts[1])
    proj_bias_grad = jnp.sum(branch_grad.astype(jnp.float32), axis=0)
    attended_grad = times_transposed(branch_grad, proj_mat)
    attended_grad = attended_grad.astype(bf16).reshape(images_here, SEQ, head_count, HD)
    scores_again = (
        jnp.einsum("iqhd,ikhd->ihqk", queries, keys_all, preferred_element_type=jnp.float32)
        * score_scale
    )
    probs_again = jnp.exp(scores_again - row_lse)
    probs_again_low = probs_again.astype(bf16)
    prob_grad = jnp.einsum(
        "iqhd,ikhd->ihqk", attended_grad, values_all, preferred_element_type=jnp.float32
    )
    value_grad = jnp.einsum(
        "ihqk,iqhd->ikhd", probs_again_low, attended_grad, preferred_element_type=jnp.float32
    )
    inner_sum = jnp.sum(prob_grad * probs_again, axis=-1, keepdims=True)
    score_grad = (probs_again * (prob_grad - inner_sum)).astype(bf16)
    query_grad = (
        jnp.einsum("ihqk,ikhd->iqhd", score_grad, keys_all, preferred_element_type=jnp.float32)
        * score_scale
    )
    key_grad = (
        jnp.einsum("ihqk,iqhd->ikhd", score_grad, queries, preferred_element_type=jnp.float32)
        * score_scale
    )
    projected_grad = jnp.concatenate(
        [
            query_grad.reshape(row_count, model_width),
            key_grad.reshape(row_count, model_width),
            value_grad.reshape(row_count, model_width),
        ],
        axis=1,
    ).astype(bf16)
    qkv_total = by_columns(normed_low, projected_grad, parts[0])
    normed_grad = times_transposed(projected_grad, qkv_mat)
    joined_from_norm, gain_first_grad, offset_first_grad = norm_back(normed_grad)
    joined_grad = (middle_grad + joined_from_norm).astype(bf16)
    skip_blocks = inner_rows(stacked, joined_grad).astype(bf16).reshape(4, 4, 2, 2 * rows, model_width)
    skip_total = fold_rows(skip_blocks, chip, core)
    skip_bias_grad = jnp.sum(joined_grad.astype(jnp.float32), axis=0)
    both_grads = times_transposed(joined_grad, skip_mat)
    input_grad = both_grads[:, :model_width]
    skip_grad = both_grads[:, model_width:]
    gain_grads = jnp.stack([gain_first_grad, gain_mid_grad])
    bias_grads = jnp.stack(
        [skip_bias_grad, offset_first_grad, proj_bias_grad, offset_mid_grad, down_bias_grad]
    )
    gains_grad, biases_grad, up_bias_total = vector_total(gain_grads, bias_grads, up_bias_grad, device)
    return (
        block_output.astype(bf16),
        input_grad,
        skip_grad,
        skip_total,
        qkv_total,
        proj_total,
        up_total,
        down_total,
        gains_grad,
        biases_grad,
        up_bias_total,
    )


def solution(mesh):
    fast = dict(mesh.shape) == {"wide": 8, "narrow": 4}
    return jax.shard_map(
        fast_shards if fast else shards,
        mesh=mesh,
        in_specs=(
            P(("wide", "narrow"), None),
            P(("wide", "narrow"), None),
            P(("wide", "narrow"), None),
            P(("wide", "narrow")),
            P(("wide", "narrow")),
            P(("wide", "narrow")),
            P(("wide", "narrow")),
            P(("wide", "narrow")),
            P(None, "narrow"),
            P(None, "narrow"),
            P("narrow"),
        ),
        out_specs=(
            P(("wide", "narrow"), None),
            P(("wide", "narrow"), None),
            P(("wide", "narrow"), None),
            P(("wide", "narrow")),
            P(("wide", "narrow")),
            P(("wide", "narrow")),
            P(("wide", "narrow")),
            P(("wide", "narrow")),
            P(None, "narrow"),
            P(None, "narrow"),
            P("narrow"),
        ),
        check_vma=False,
    )
```
